512 devices in a mesh: group: 16 (over z), shard: 32 (over y, x, core).
Axes of the slice: x: 4, y: 4, z: 16, core: 2. Of those that a mesh axis runs over, the one named last changes fastest.
Arguments:
- entry_grads: float32 [16, 32, 256, 1280], P('group', 'shard'), may hold values from -800 to 800
- exit_grads: float32 [16, 32, 256, 1024], P('group', 'shard'), may hold values from -800 to 800
- entry_params: float32 [32, 256, 1280], P('shard', 'group'), may hold values from -0.15625 to 0.15625
- exit_params: float32 [32, 256, 1024], P('shard', 'group'), may hold values from -0.15625 to 0.15625
- entry_mean: float32 [32, 256, 1280], P('shard', 'group'), may hold values from -1.5 to 1.5
- exit_mean: float32 [32, 256, 1024], P('shard', 'group'), may hold values from -1.5 to 1.5
- entry_square: float32 [32, 256, 1280], P('shard', 'group'), may hold values from 0.01 to 1
- exit_square: float32 [32, 256, 1024], P('shard', 'group'), may hold values from 0.01 to 1
Outputs:
- entry_master: float32 [32, 256, 1280], P('shard', 'group')
- exit_master: float32 [32, 256, 1024], P('shard', 'group')
- entry_moment: float32 [32, 256, 1280], P('shard', 'group')
- exit_moment: float32 [32, 256, 1024], P('shard', 'group')
- entry_variance: float32 [32, 256, 1280], P('shard', 'group')
- exit_variance: float32 [32, 256, 1024], P('shard', 'group')
- entry_weights: bfloat16 [32, 256, 1280], P('shard')
- exit_weights: bfloat16 [32, 256, 1024], P('shard')
The draws below stay inside these ranges and needn't reach their ends.
All inputs are finite; a program needn't handle non-finite values.
Results may differ from the reference program's by a relative error of at most 0.0004.
Values may be sent and summed in bfloat16 or wider, within the bound.
No kernel may reach another device: no remote copies, remote signals or barrier semaphores. Data moves between devices by JAX's collectives and lax.ppermute only.
A program may use at most 64 MiB of HBM per device.

```python
import math
import jax
import jax.numpy as jnp
from jax import lax

Q_DEV = 256
O_DEV = 256
QKV_COLS = 1280
O_COLS = 1024
GROUPS = 16
SHARDS = 32
NUMEL = 18874368


def shard_amplitude(key):
    keys = jax.random.split(key, 4)
    half_count = SHARDS // 2
    top_count = min(4, half_count)
    parity = jax.random.randint(keys[0], (), 0, 2).astype(jnp.int32)
    hot_shards = parity + 2 * jax.random.permutation(keys[1], half_count).astype(jnp.int32)
    cold_shards = 1 - parity + 2 * jax.random.permutation(keys[2], half_count).astype(jnp.int32)
    others = jax.random.permutation(keys[3], jnp.concatenate([hot_shards[top_count:], cold_shards]))
    ordering = jnp.concatenate([hot_shards[:top_count], others]).astype(jnp.int32)
    ranking = jnp.zeros((SHARDS,), jnp.int32).at[ordering].set(jnp.arange(SHARDS, dtype=jnp.int32))
    spread = ranking.astype(jnp.float32) / float(max(SHARDS - 1, 1))
    return jnp.exp(-spread * math.log(100.0))


def gradient_draw(key, rows, width):
    keys = jax.random.split(key, 5)
    shape = (GROUPS, SHARDS, rows, width)
    base = jnp.clip(jax.random.normal(keys[0], shape, jnp.float32), -6.0, 6.0)
    position = (jnp.arange(SHARDS, dtype=jnp.float32)[:, None] * rows + jnp.arange(rows, dtype=jnp.float32)[None, :]) / (SHARDS * rows)
    rising = (3.0 ** position)[None, :, :, None]
    rough = jnp.exp(jax.random.uniform(keys[1], (GROUPS, SHARDS, rows, 1), jnp.float32, 0.0, math.log(10.0)))
    column = jnp.exp(jax.random.uniform(keys[2], (1, 1, 1, width), jnp.float32, 0.0, math.log(10.0)))
    amplitude = shard_amplitude(keys[4])[None, :, None, None]
    return (base * rising * rough * column * amplitude * 0.1).astype(jnp.float32)


def draw_entry_grads(key, part):
    return gradient_draw(jax.random.fold_in(key, 11), Q_DEV, QKV_COLS)


def draw_exit_grads(key, part):
    return gradient_draw(jax.random.fold_in(key, 23), O_DEV, O_COLS)


def shard_levels(own_key, shape, pieces, least, high):
    loudness, own = 1.0, jax.random.fold_in(own_key, 6)
    for dim, shards_of in pieces:
        draws = jnp.exp(jax.random.uniform(jax.random.fold_in(own, dim), (shards_of,), jnp.float32, least / len(pieces), high / len(pieces)))
        loudness = loudness * jnp.repeat(draws, shape[dim] // shards_of).reshape([-1 if axis == dim else 1 for axis in range(len(shape))])
    return loudness


def normal_values(rng, dims, scale, most, cuts=(), kind=jnp.bfloat16):
    values = scale * jax.random.normal(rng, dims, jnp.float32)
    if cuts:
        values = values * shard_levels(rng, dims, cuts, -0.22, 0.18)
    return jnp.clip(values, -most, most).astype(kind)


def setup_inputs(seed: int = 0) -> dict:
    key_list = jax.random.split(jax.random.key(seed), 9)
    entry_grads = draw_entry_grads(jax.random.fold_in(key_list[8], 71), 0)
    exit_grads = draw_exit_grads(jax.random.fold_in(key_list[8], 71), 0)
    entry_params = normal_values(key_list[2], (SHARDS, Q_DEV, QKV_COLS), 0.01, 0.15625, ((0, 32), (1, 16)), jnp.float32)
    exit_params = normal_values(key_list[3], (SHARDS, O_DEV, O_COLS), 0.01, 0.15625, ((0, 32), (1, 16)), jnp.float32)
    entry_mean = normal_values(key_list[4], (SHARDS, Q_DEV, QKV_COLS), 0.1, 1.5, ((0, 32), (1, 16)), jnp.float32)
    exit_mean = normal_values(key_list[5], (SHARDS, O_DEV, O_COLS), 0.1, 1.5, ((0, 32), (1, 16)), jnp.float32)
    entry_square = jnp.clip(jnp.exp(math.log(1.0) - 4.6051702 * jax.random.uniform(key_list[6], (SHARDS, Q_DEV, QKV_COLS), jnp.float32) ** shard_levels(key_list[6], (SHARDS, Q_DEV, QKV_COLS), ((0, 32), (1, 16)), -0.2, 0.2)), 0.01, 1.0)
    exit_square = jnp.clip(jnp.exp(math.log(1.0) - 4.6051702 * jax.random.uniform(key_list[7], (SHARDS, O_DEV, O_COLS), jnp.float32) ** shard_levels(key_list[7], (SHARDS, O_DEV, O_COLS), ((0, 32), (1, 16)), -0.2, 0.2)), 0.01, 1.0)
    return {"entry_grads": entry_grads, "exit_grads": exit_grads, "entry_params": entry_params, "exit_params": exit_params, "entry_mean": entry_mean, "exit_mean": exit_mean, "entry_square": entry_square, "exit_square": exit_square}


beta_first = 0.9
beta_second = 0.95
learn_rate = 0.01
decay_rate = 0.1
epsilon = 1e-08
correct_first = 1.0 - 0.9 ** 40
correct_second = 1.0 - 0.95 ** 40

def adamw_step(params, mean, square, total, clip):
    grads = clip * total
    moment = beta_first * mean + (1.0 - beta_first) * grads
    variance = beta_second * square + (1.0 - beta_second) * grads * grads
    update = moment / correct_first / (jnp.sqrt(variance / correct_second) + epsilon)
    master = params - learn_rate * (update + decay_rate * params)
    return (master, moment, variance)

def reference(entry_grads, exit_grads, entry_params, exit_params, entry_mean, exit_mean, entry_square, exit_square):
    entry_total = lax.optimization_barrier(jnp.sum(entry_grads, axis=0, dtype=jnp.float32))
    exit_total = lax.optimization_barrier(jnp.sum(exit_grads, axis=0, dtype=jnp.float32))
    squares = jnp.sum(entry_total * entry_total) + jnp.sum(exit_total * exit_total)
    grad_norm = jnp.sqrt(squares)
    limit = jnp.sqrt(jnp.float32(NUMEL))
    clip = jnp.minimum(jnp.float32(1.0), limit / (grad_norm + 1e-06))
    entry_master, entry_moment, entry_variance = adamw_step(entry_params, entry_mean, entry_square, entry_total, clip)
    exit_master, exit_moment, exit_variance = adamw_step(exit_params, exit_mean, exit_square, exit_total, clip)
    return (entry_master, exit_master, entry_moment, exit_moment, entry_variance, exit_variance, entry_master.astype(jnp.bfloat16), exit_master.astype(jnp.bfloat16))
```

```python
import jax
import jax.numpy as jnp
from jax import lax
from jax.sharding import PartitionSpec as P

beta_first = 0.9
beta_second = 0.95
learn_rate = 0.01
decay_rate = 0.1
epsilon = 1e-08
correct_first = 1.0 - 0.9**40
correct_second = 1.0 - 0.95**40


def adamw_step(params, mean, square, total, clip):
    grads = clip * total
    moment = beta_first * mean + (1.0 - beta_first) * grads
    variance = beta_second * square + (1.0 - beta_second) * grads * grads
    update = moment / correct_first / (jnp.sqrt(variance / correct_second) + epsilon)
    master = params - learn_rate * (update + decay_rate * params)
    return (master, moment, variance)


def sum_everywhere(values):
    axes = ("group", "shard")
    lanes = jnp.sum(values.reshape(-1, 128), axis=0)
    sent = jnp.broadcast_to(lanes, (lax.axis_size(axes), 1, 128))
    return jnp.sum(lax.all_to_all(sent, axes, 0, 0))


def body(
    entry_grads,
    exit_grads,
    entry_params,
    exit_params,
    entry_mean,
    exit_mean,
    entry_square,
    exit_square,
):
    entry_rows_dev = entry_grads.shape[2]
    exit_rows_dev = exit_grads.shape[2]
    entry_width = entry_grads.shape[3]
    exit_width = exit_grads.shape[3]
    entry_local = entry_grads.reshape(entry_rows_dev, entry_width)
    exit_local = exit_grads.reshape(exit_rows_dev, exit_width)
    packed = jnp.concatenate([entry_local, exit_local], axis=1)
    total = lax.psum_scatter(packed, "group", scatter_dimension=0, tiled=True)
    entry_total = total[:, :entry_width]
    exit_total = total[:, entry_width:]
    squares = sum_everywhere(total * total)
    count = (entry_rows_dev * entry_width + exit_rows_dev * exit_width) * lax.axis_size("shard")
    limit = jnp.sqrt(jnp.float32(count))
    clip = jnp.minimum(jnp.float32(1.0), limit / (jnp.sqrt(squares) + 1e-06))
    entry_master, entry_moment, entry_variance = adamw_step(
        entry_params[0], entry_mean[0], entry_square[0], entry_total, clip
    )
    exit_master, exit_moment, exit_variance = adamw_step(
        exit_params[0], exit_mean[0], exit_square[0], exit_total, clip
    )
    entry_round = entry_master.astype(jnp.bfloat16)
    exit_round = exit_master.astype(jnp.bfloat16)
    entry_weights = lax.all_gather(entry_round, "group", axis=0, tiled=True)
    exit_weights = lax.all_gather(exit_round, "group", axis=0, tiled=True)
    return (
        entry_master[None],
        exit_master[None],
        entry_moment[None],
        exit_moment[None],
        entry_variance[None],
        exit_variance[None],
        entry_weights[None],
        exit_weights[None],
    )


def solution(mesh):
    placed = (
        P("group", "shard", None, None),
        P("group", "shard", None, None),
        P("shard", "group", None),
        P("shard", "group", None),
        P("shard", "group", None),
        P("shard", "group", None),
        P("shard", "group", None),
        P("shard", "group", None),
    )
    return jax.shard_map(
        body,
        mesh=mesh,
        in_specs=placed,
        out_specs=(
            P("shard", "group", None),
            P("shard", "group", None),
            P("shard", "group", None),
            P("shard", "group", None),
            P("shard", "group", None),
            P("shard", "group", None),
            P("shard", None, None),
            P("shard", None, None),
        ),
        check_vma=False,
    )
```

```python
import jax
import jax.numpy as jnp
from jax import lax
from jax.experimental import pallas as pl
from jax.experimental.pallas import tpu as pltpu
from jax.sharding import PartitionSpec as P

beta_first = 0.9
beta_second = 0.95
learn_rate = 0.01
decay_rate = 0.1
epsilon = 1e-08
correct_first = 1.0 - 0.9**40
correct_second = 1.0 - 0.95**40

LANES = 128
TILE = 8
ENTRY_PIECE = 640
EXIT_PIECE = 1024


def adamw_step(params, mean, square, total, clip):
    grads = clip * total
    moment = beta_first * mean + (1.0 - beta_first) * grads
    variance = beta_second * square + (1.0 - beta_second) * grads * grads
    update = moment / correct_first / (jnp.sqrt(variance / correct_second) + epsilon)
    master = params - learn_rate * (update + decay_rate * params)
    return (master, moment, variance)


def pieces_of(grads, width):
    rows, cols = grads.shape
    return [
        grads[r : r + TILE, c : c + width]
        for r in range(0, rows, TILE)
        for c in range(0, cols, width)
    ]


def join_kernel(places, *refs):
    piece_refs, (total_ref, lanes_ref) = refs[: len(places)], refs[len(places) :]
    sums = [jnp.zeros((TILE, LANES), jnp.float32) for _ in range(4)]
    turn = 0
    for (row, col), piece_ref in zip(places, piece_refs):
        for c in range(0, piece_ref.shape[1], LANES):
            values = piece_ref[:, c : c + LANES]
            total_ref[row : row + TILE, col + c : col + c + LANES] = values
            sums[turn % 4] = sums[turn % 4] + values * values
            turn += 1
    sums = (sums[0] + sums[1]) + (sums[2] + sums[3])
    lanes_ref[...] = jnp.sum(sums, axis=0, keepdims=True)


def join(entry_pieces, exit_pieces, rows, entry_width, exit_width):
    places = [(r, c) for r in range(0, rows, TILE) for c in range(0, entry_width, ENTRY_PIECE)]
    places += [
        (r, entry_width + c) for r in range(0, rows, TILE) for c in range(0, exit_width, EXIT_PIECE)
    ]
    return pl.pallas_call(
        lambda *refs: join_kernel(places, *refs),
        out_shape=(
            jax.ShapeDtypeStruct((rows, entry_width + exit_width), jnp.float32),
            jax.ShapeDtypeStruct((1, LANES), jnp.float32),
        ),
        name="join_totals",
    )(*entry_pieces, *exit_pieces)


def weights_kernel(rows, entry_width, scale_ref, state_ref, total_ref, entry_ref, exit_ref):
    along, squared = scale_ref[0, 0], scale_ref[0, 1]
    step = 2 * LANES
    for part in range(total_ref.shape[0] // rows):
        here = slice(part * rows, (part + 1) * rows)
        top = part * 3 * rows
        for c in range(0, total_ref.shape[1], step):
            cols = slice(c, c + step)
            total = total_ref[here, cols]
            ahead = state_ref[top + rows : top + 2 * rows, cols] + along * total
            spread = state_ref[top + 2 * rows : top + 3 * rows, cols] + squared * (total * total)
            master = state_ref[top : top + rows, cols] - ahead / (jnp.sqrt(spread) + epsilon)
            out_ref, at = (entry_ref, c) if c < entry_width else (exit_ref, c - entry_width)
            out_ref[here, at : at + step] = master.astype(out_ref.dtype)


def weights(scales, state, total, rows, entry_width, exit_width, parts):
    groups = total.shape[0] // rows
    high = rows * parts
    return pl.pallas_call(
        lambda *refs: weights_kernel(rows, entry_width, *refs),
        grid=(groups // parts,),
        in_specs=[
            pl.BlockSpec(memory_space=pltpu.SMEM),
            pl.BlockSpec((3 * high, total.shape[1]), lambda i: (i, 0)),
            pl.BlockSpec((high, total.shape[1]), lambda i: (i, 0)),
        ],
        out_specs=[
            pl.BlockSpec((high, entry_width), lambda i: (i, 0)),
            pl.BlockSpec((high, exit_width), lambda i: (i, 0)),
        ],
        out_shape=[
            jax.ShapeDtypeStruct((total.shape[0], entry_width), jnp.bfloat16),
            jax.ShapeDtypeStruct((total.shape[0], exit_width), jnp.bfloat16),
        ],
        name="all_weights",
    )(scales, state, total)


def body(
    entry_grads,
    exit_grads,
    entry_params,
    exit_params,
    entry_mean,
    exit_mean,
    entry_square,
    exit_square,
):
    rows, entry_width = entry_grads.shape[2:]
    exit_width = exit_grads.shape[3]
    own = entry_params.shape[1]
    state = jnp.concatenate(
        [
            jnp.concatenate([entry_params[0], exit_params[0]], 1) * (1.0 - learn_rate * decay_rate),
            jnp.concatenate([entry_mean[0], exit_mean[0]], 1)
            * (learn_rate * beta_first / correct_first),
            jnp.concatenate([entry_square[0], exit_square[0]], 1) * (beta_second / correct_second),
        ],
        axis=0,
    )
    all_state = lax.all_gather(state, "group", axis=0, tiled=True)

    entry_pieces = pieces_of(entry_grads.reshape(rows, entry_width), ENTRY_PIECE)
    exit_pieces = pieces_of(exit_grads.reshape(rows, exit_width), EXIT_PIECE)
    summed = lax.psum(entry_pieces + exit_pieces, "group")
    total, lanes = join(
        summed[: len(entry_pieces)], summed[len(entry_pieces) :], rows, entry_width, exit_width
    )
    shards = lax.axis_size("shard")
    sent = jnp.broadcast_to(lanes, (shards, 1, LANES))
    squares = jnp.sum(lax.all_to_all(sent, "shard", 0, 0))
    count = (rows * entry_width + rows * exit_width) * shards
    limit = jnp.sqrt(jnp.float32(count))
    clip = jnp.minimum(jnp.float32(1.0), limit / (jnp.sqrt(squares) + 1e-06))

    first = lax.axis_index("group") * own
    mine = lax.dynamic_slice_in_dim(total, first, own, axis=0)
    entry_master, entry_moment, entry_variance = adamw_step(
        entry_params[0], entry_mean[0], entry_square[0], mine[:, :entry_width], clip
    )
    exit_master, exit_moment, exit_variance = adamw_step(
        exit_params[0], exit_mean[0], exit_square[0], mine[:, entry_width:], clip
    )
    along = clip * (learn_rate * (1.0 - beta_first) / correct_first)
    squared = clip * clip * ((1.0 - beta_second) / correct_second)
    scales = jnp.stack([along, squared]).reshape(1, 2)
    entry_weights, exit_weights = weights(
        scales, all_state, total, own, entry_width, exit_width, parts=2
    )
    return (
        entry_master[None],
        exit_master[None],
        entry_moment[None],
        exit_moment[None],
        entry_variance[None],
        exit_variance[None],
        entry_weights[None],
        exit_weights[None],
    )


def solution(mesh):
    placed = (
        P("group", "shard", None, None),
        P("group", "shard", None, None),
        P("shard", "group", None),
        P("shard", "group", None),
        P("shard", "group", None),
        P("shard", "group", None),
        P("shard", "group", None),
        P("shard", "group", None),
    )
    return jax.shard_map(
        body,
        mesh=mesh,
        in_specs=placed,
        out_specs=(
            P("shard", "group", None),
            P("shard", "group", None),
            P("shard", "group", None),
            P("shard", "group", None),
            P("shard", "group", None),
            P("shard", "group", None),
            P("shard", None, None),
            P("shard", None, None),
        ),
        check_vma=False,
    )
```

```python
import jax
import jax.numpy as jnp
from jax import lax
from jax.experimental import pallas as pl
from jax.experimental.pallas import tpu as pltpu
from jax.sharding import PartitionSpec as P

beta_first = 0.9
beta_second = 0.95
learn_rate = 0.01
decay_rate = 0.1
epsilon = 1e-08
correct_first = 1.0 - 0.9**40
correct_second = 1.0 - 0.95**40

LANES = 128
TILE = 8
ENTRY_PIECE = 640
EXIT_PIECE = 1024
NEAR = 4


def pieces_of(grads, width):
    rows, cols = grads.shape
    return [
        grads[r : r + TILE, c : c + width]
        for r in range(0, rows, TILE)
        for c in range(0, cols, width)
    ]


def places_of(rows, cols, width, start):
    return [(r, start + c) for r in range(0, rows, TILE) for c in range(0, cols, width)]


def own_and_squares_kernel(places, own, me_ref, *refs):
    piece_refs, (own_ref, lanes_ref) = refs[: len(places)], refs[len(places) :]
    me = me_ref[0, 0]
    sums = [jnp.zeros((TILE, LANES), jnp.float32) for _ in range(4)]
    turn = 0
    for piece_ref in piece_refs:
        for c in range(0, piece_ref.shape[1], LANES):
            values = piece_ref[:, c : c + LANES]
            sums[turn % 4] = sums[turn % 4] + values * values
            turn += 1
    sums = (sums[0] + sums[1]) + (sums[2] + sums[3])
    lanes = jnp.sum(sums, axis=0, keepdims=True)
    lanes_ref[...] = jnp.broadcast_to(lanes[None], lanes_ref.shape)
    for block in sorted({row // own for row, _ in places}):

        @pl.when(me == block)
        def _(block=block):
            for (row, col), piece_ref in zip(places, piece_refs):
                if row // own == block:
                    top = row - block * own
                    own_ref[top : top + TILE, col : col + piece_ref.shape[1]] = piece_ref[...]


def own_and_squares(pieces, places, own, width, shards):
    me = lax.axis_index("group").reshape(1, 1)
    return pl.pallas_call(
        lambda *refs: own_and_squares_kernel(places, own, *refs),
        in_specs=[pl.BlockSpec(memory_space=pltpu.SMEM)]
        + [pl.BlockSpec(memory_space=pltpu.VMEM) for _ in pieces],
        out_shape=(
            jax.ShapeDtypeStruct((own, width), jnp.float32),
            jax.ShapeDtypeStruct((shards, 1, LANES), jnp.float32),
        ),
        name="own_and_squares",
    )(me, *pieces)


def update_kernel(limit, entry_width, refs):
    squares_ref, total_ref = refs[:2]
    states, outs, round_ref = refs[2:8], refs[8:14], refs[14]
    squares = jnp.sum(jnp.sum(squares_ref[...], axis=0), axis=1, keepdims=True)
    clip = jnp.minimum(jnp.float32(1.0), limit / (jnp.sqrt(squares) + 1e-06))
    for side, start in ((0, 0), (1, entry_width)):
        params_ref, mean_ref, square_ref = states[side], states[2 + side], states[4 + side]
        for c in range(0, params_ref.shape[2], 2 * LANES):
            cols = slice(c, c + 2 * LANES)
            there = slice(start + c, start + c + 2 * LANES)
            params = params_ref[0, :, cols]
            grads = clip * total_ref[:, there]
            moment = beta_first * mean_ref[0, :, cols] + (1.0 - beta_first) * grads
            variance = beta_second * square_ref[0, :, cols] + (1.0 - beta_second) * grads * grads
            update = moment / correct_first / (jnp.sqrt(variance / correct_second) + epsilon)
            master = params - learn_rate * (update + decay_rate * params)
            outs[side][0, :, cols] = master
            outs[2 + side][0, :, cols] = moment
            outs[4 + side][0, :, cols] = variance
            round_ref[:, there] = master.astype(round_ref.dtype)


def update(squares, total, states, limit, entry_width):
    return pl.pallas_call(
        lambda *refs: update_kernel(limit, entry_width, refs),
        out_shape=[jax.ShapeDtypeStruct(s.shape, s.dtype) for s in states]
        + [jax.ShapeDtypeStruct(total.shape, jnp.bfloat16)],
        name="own_update",
    )(squares, total, *states)


def place_kernel(own, entry_width, me_ref, own_ref, ahead_ref, across_ref, after_ref, behind_ref, entry_ref, exit_ref):
    me = me_ref[0, 0]
    half = across_ref.shape[1]
    for residue in range(NEAR):
        for turn in range(NEAR):

            @pl.when(lax.rem(me + turn, NEAR) == residue)
            def _(residue=residue, turn=turn):
                for block in range(own_ref.shape[0] // own):
                    src = slice(block * own, (block + 1) * own)
                    top = (block * NEAR + residue) * own
                    dst = slice(top, top + own)
                    for out_ref, start in ((entry_ref, 0), (exit_ref, entry_width)):
                        end = start + out_ref.shape[1]
                        if turn != 2:
                            ref = (own_ref, ahead_ref, None, behind_ref)[turn]
                            out_ref[dst, :] = ref[src, start:end]
                            continue
                        if start < half:
                            stop = min(half, end)
                            out_ref[dst, : stop - start] = across_ref[src, start:stop]
                        if end > half:
                            low = max(half, start)
                            out_ref[dst, low - start :] = after_ref[src, low - half : end - half]


def share(rounded, entry_width):
    groups = lax.axis_size("group")
    own, width = rounded.shape
    far = groups // NEAR
    half = width // 2
    strides = [[r + NEAR * a for a in range(far)] for r in range(NEAR)]
    gathered = lax.all_gather(rounded, "group", axis=0, tiled=True, axis_index_groups=strides)

    def moved(values, by):
        return lax.ppermute(values, "group", [(i, (i + by) % groups) for i in range(groups)])

    ahead, behind = moved(gathered, -1), moved(gathered, 1)
    across, after = moved(gathered[:, :half], 2), moved(gathered[:, half:], -2)
    me = lax.axis_index("group").reshape(1, 1)
    vmem = pl.BlockSpec(memory_space=pltpu.VMEM)
    return pl.pallas_call(
        lambda *refs: place_kernel(own, entry_width, *refs),
        in_specs=[pl.BlockSpec(memory_space=pltpu.SMEM)] + [vmem] * 5,
        out_shape=[
            jax.ShapeDtypeStruct((groups * own, entry_width), rounded.dtype),
            jax.ShapeDtypeStruct((groups * own, width - entry_width), rounded.dtype),
        ],
        name="place_weights",
    )(me, gathered, ahead, across, after, behind)


def body(
    entry_grads,
    exit_grads,
    entry_params,
    exit_params,
    entry_mean,
    exit_mean,
    entry_square,
    exit_square,
):
    rows, entry_width = entry_grads.shape[2:]
    exit_width = exit_grads.shape[3]
    own = entry_params.shape[1]
    shards = lax.axis_size("shard")
    pieces = pieces_of(entry_grads.reshape(rows, entry_width), ENTRY_PIECE)
    pieces += pieces_of(exit_grads.reshape(rows, exit_width), EXIT_PIECE)
    places = places_of(rows, entry_width, ENTRY_PIECE, 0)
    places += places_of(rows, exit_width, EXIT_PIECE, entry_width)
    summed = lax.psum(pieces, "group")
    total, lanes = own_and_squares(summed, places, own, entry_width + exit_width, shards)
    squares = lax.all_to_all(lanes, "shard", 0, 0)
    limit = ((rows * entry_width + rows * exit_width) * shards) ** 0.5
    states = (entry_params, exit_params, entry_mean, exit_mean, entry_square, exit_square)
    *outs, rounded = update(squares, total, states, limit, entry_width)
    entry_weights, exit_weights = share(rounded, entry_width)
    return (*outs, entry_weights[None], exit_weights[None])


def solution(mesh):
    placed = (
        P("group", "shard", None, None),
        P("group", "shard", None, None),
        P("shard", "group", None),
        P("shard", "group", None),
        P("shard", "group", None),
        P("shard", "group", None),
        P("shard", "group", None),
        P("shard", "group", None),
    )
    return jax.shard_map(
        body,
        mesh=mesh,
        in_specs=placed,
        out_specs=(
            P("shard", "group", None),
            P("shard", "group", None),
            P("shard", "group", None),
            P("shard", "group", None),
            P("shard", "group", None),
            P("shard", "group", None),
            P("shard", None, None),
            P("shard", None, None),
        ),
        check_vma=False,
    )
```

```python
import jax
import jax.numpy as jnp
from jax import lax
from jax.experimental import pallas as pl
from jax.experimental.pallas import tpu as pltpu
from jax.sharding import PartitionSpec as P

beta_first = 0.9
beta_second = 0.95
learn_rate = 0.01
decay_rate = 0.1
epsilon = 1e-08
correct_first = 1.0 - 0.9**40
correct_second = 1.0 - 0.95**40

LANES = 128
TILE = 8
ENTRY_PIECE = 640
EXIT_PIECE = 1024
NEAR = 4


def pieces_of(grads, width):
    rows, cols = grads.shape
    return [
        grads[r : r + TILE, c : c + width]
        for r in range(0, rows, TILE)
        for c in range(0, cols, width)
    ]


def places_of(rows, cols, width, start):
    return [(r, start + c) for r in range(0, rows, TILE) for c in range(0, cols, width)]


def own_and_squares_kernel(places, own, me_ref, *refs):
    piece_refs, (own_ref, lanes_ref) = refs[: len(places)], refs[len(places) :]
    me = me_ref[0, 0]
    sums = [jnp.zeros((TILE, LANES), jnp.float32) for _ in range(4)]
    turn = 0
    for piece_ref in piece_refs:
        for c in range(0, piece_ref.shape[1], LANES):
            values = piece_ref[:, c : c + LANES]
            sums[turn % 4] = sums[turn % 4] + values * values
            turn += 1
    sums = (sums[0] + sums[1]) + (sums[2] + sums[3])
    lanes = jnp.sum(sums, axis=0, keepdims=True)
    lanes_ref[...] = jnp.broadcast_to(lanes[None], lanes_ref.shape)
    for block in sorted({row // own for row, _ in places}):

        @pl.when(me == block)
        def _(block=block):
            for (row, col), piece_ref in zip(places, piece_refs):
                if row // own == block:
                    top = row - block * own
                    own_ref[top : top + TILE, col : col + piece_ref.shape[1]] = piece_ref[...]


def own_and_squares(pieces, places, own, width, shards):
    me = lax.axis_index("group").reshape(1, 1)
    return pl.pallas_call(
        lambda *refs: own_and_squares_kernel(places, own, *refs),
        in_specs=[pl.BlockSpec(memory_space=pltpu.SMEM)]
        + [pl.BlockSpec(memory_space=pltpu.VMEM) for _ in pieces],
        out_shape=(
            jax.ShapeDtypeStruct((own, width), jnp.float32),
            jax.ShapeDtypeStruct((shards, 1, LANES), jnp.float32),
        ),
        name="own_and_squares",
    )(me, *pieces)


def clip_of(squares_ref, limit):
    squares = jnp.sum(jnp.sum(squares_ref[...], axis=0), axis=1, keepdims=True)
    return jnp.minimum(jnp.float32(1.0), limit / (jnp.sqrt(squares) + 1e-06))


def adamw_step(params, mean, square, total, clip):
    grads = clip * total
    moment = beta_first * mean + (1.0 - beta_first) * grads
    variance = beta_second * square + (1.0 - beta_second) * grads * grads
    update = moment / correct_first / (jnp.sqrt(variance / correct_second) + epsilon)
    master = params - learn_rate * (update + decay_rate * params)
    return (master, moment, variance)


def update_kernel(limit, entry_width, keep, refs):
    squares_ref, total_ref = refs[:2]
    states, outs = refs[2:8], refs[8:]
    clip = clip_of(squares_ref, limit)
    for side, start in ((0, 0), (1, entry_width)):
        params_ref, mean_ref, square_ref = states[side], states[2 + side], states[4 + side]
        for c in range(0, params_ref.shape[2], 2 * LANES):
            cols = slice(c, c + 2 * LANES)
            there = slice(start + c, start + c + 2 * LANES)
            stepped = adamw_step(
                params_ref[0, :, cols],
                mean_ref[0, :, cols],
                square_ref[0, :, cols],
                total_ref[:, there],
                clip,
            )
            if keep:
                for kind, values in enumerate(stepped):
                    outs[2 * kind + side][0, :, cols] = values
            else:
                outs[0][:, there] = stepped[0].astype(outs[0].dtype)


def update(squares, total, states, limit, entry_width, keep):
    if keep:
        shapes = [jax.ShapeDtypeStruct(s.shape, s.dtype) for s in states]
    else:
        shapes = [jax.ShapeDtypeStruct(total.shape, jnp.bfloat16)]
    return pl.pallas_call(
        lambda *refs: update_kernel(limit, entry_width, keep, refs),
        out_shape=shapes,
        name="own_state" if keep else "own_weights",
    )(squares, total, *states)


def share(rounded, entry_width):
    groups = lax.axis_size("group")
    own, width = rounded.shape
    far = groups // NEAR
    strides = [[r + NEAR * a for a in range(far)] for r in range(NEAR)]
    gathered = lax.all_gather(rounded, "group", axis=0, tiled=True, axis_index_groups=strides)

    def moved(values, by):
        return lax.ppermute(values, "group", [(i, (i + by) % groups) for i in range(groups)])

    ahead, behind = moved(gathered, -1), moved(gathered, 1)
    across = (moved(gathered[:, :entry_width], 2), moved(gathered[:, entry_width:], -2))
    me = lax.axis_index("group").astype(jnp.uint32)

    def placed(nearby, cols):
        shape = (far, NEAR, own, cols)
        residue = lax.broadcasted_iota(jnp.uint32, shape, 1)
        out = nearby[0].reshape(far, 1, own, cols)
        for turn in range(1, NEAR):
            here = residue == ((me + turn) & (NEAR - 1))
            out = jnp.where(here, nearby[turn].reshape(far, 1, own, cols), out)
        return out.reshape(groups * own, cols)

    sides = ((slice(0, entry_width), across[0]), (slice(entry_width, width), across[1]))
    return gathered, [
        placed((gathered[:, cols], ahead[:, cols], middle, behind[:, cols]), middle.shape[1])
        for cols, middle in sides
    ]


def body(
    entry_grads,
    exit_grads,
    entry_params,
    exit_params,
    entry_mean,
    exit_mean,
    entry_square,
    exit_square,
):
    rows, entry_width = entry_grads.shape[2:]
    exit_width = exit_grads.shape[3]
    own = entry_params.shape[1]
    shards = lax.axis_size("shard")
    pieces = pieces_of(entry_grads.reshape(rows, entry_width), ENTRY_PIECE)
    pieces += pieces_of(exit_grads.reshape(rows, exit_width), EXIT_PIECE)
    places = places_of(rows, entry_width, ENTRY_PIECE, 0)
    places += places_of(rows, exit_width, EXIT_PIECE, entry_width)
    summed = lax.psum(pieces, "group")
    total, lanes = own_and_squares(summed, places, own, entry_width + exit_width, shards)
    squares = lax.all_to_all(lanes, "shard", 0, 0)
    limit = ((rows * entry_width + rows * exit_width) * shards) ** 0.5
    states = (entry_params, exit_params, entry_mean, exit_mean, entry_square, exit_square)
    (rounded,) = update(squares, total, states, limit, entry_width, keep=False)
    gathered, (entry_weights, exit_weights) = share(rounded, entry_width)
    squares, gathered = lax.optimization_barrier((squares, gathered))
    outs = update(squares, total, states, limit, entry_width, keep=True)
    return (*outs, entry_weights[None], exit_weights[None])


def solution(mesh):
    placed = (
        P("group", "shard", None, None),
        P("group", "shard", None, None),
        P("shard", "group", None),
        P("shard", "group", None),
        P("shard", "group", None),
        P("shard", "group", None),
        P("shard", "group", None),
        P("shard", "group", None),
    )
    return jax.shard_map(
        body,
        mesh=mesh,
        in_specs=placed,
        out_specs=(
            P("shard", "group", None),
            P("shard", "group", None),
            P("shard", "group", None),
            P("shard", "group", None),
            P("shard", "group", None),
            P("shard", "group", None),
            P("shard", None, None),
            P("shard", None, None),
        ),
        check_vma=False,
    )
```

```python
import jax
import jax.numpy as jnp
from jax import lax
from jax.experimental import pallas as pl
from jax.experimental.pallas import tpu as pltpu
from jax.sharding import PartitionSpec as P

beta_first = 0.9
beta_second = 0.95
learn_rate = 0.01
decay_rate = 0.1
epsilon = 1e-08
correct_first = 1.0 - 0.9**40
correct_second = 1.0 - 0.95**40

LANES = 128
TILE = 8
ENTRY_PIECE = 640
EXIT_PIECE = 1024
NEAR = 4


def pieces_of(grads, width):
    rows, cols = grads.shape
    return [
        grads[r : r + TILE, c : c + width]
        for r in range(0, rows, TILE)
        for c in range(0, cols, width)
    ]


def places_of(rows, cols, width, start):
    return [(r, start + c) for r in range(0, rows, TILE) for c in range(0, cols, width)]


def own_and_squares_kernel(places, own, me_ref, *refs):
    piece_refs, (own_ref, lanes_ref) = refs[: len(places)], refs[len(places) :]
    me = me_ref[0, 0]
    sums = [jnp.zeros((TILE, LANES), jnp.float32) for _ in range(4)]
    turn = 0
    for piece_ref in piece_refs:
        for c in range(0, piece_ref.shape[1], LANES):
            values = piece_ref[:, c : c + LANES]
            sums[turn % 4] = sums[turn % 4] + values * values
            turn += 1
    sums = (sums[0] + sums[1]) + (sums[2] + sums[3])
    lanes = jnp.sum(sums, axis=0, keepdims=True)
    lanes_ref[...] = jnp.broadcast_to(lanes[None], lanes_ref.shape)
    for block in sorted({row // own for row, _ in places}):

        @pl.when(me == block)
        def _(block=block):
            for (row, col), piece_ref in zip(places, piece_refs):
                if row // own == block:
                    top = row - block * own
                    own_ref[top : top + TILE, col : col + piece_ref.shape[1]] = piece_ref[...]


def own_and_squares(pieces, places, own, width, shards):
    me = lax.axis_index("group").reshape(1, 1)
    return pl.pallas_call(
        lambda *refs: own_and_squares_kernel(places, own, *refs),
        in_specs=[pl.BlockSpec(memory_space=pltpu.SMEM)]
        + [pl.BlockSpec(memory_space=pltpu.VMEM) for _ in pieces],
        out_shape=(
            jax.ShapeDtypeStruct((own, width), jnp.float32),
            jax.ShapeDtypeStruct((shards, 1, LANES), jnp.float32),
        ),
        name="own_and_squares",
    )(me, *pieces)


def clip_of(squares_ref, limit):
    squares = jnp.sum(jnp.sum(squares_ref[...], axis=0), axis=1, keepdims=True)
    return jnp.minimum(jnp.float32(1.0), limit / (jnp.sqrt(squares) + 1e-06))


def adamw_step(params, mean, square, total, clip):
    grads = clip * total
    moment = beta_first * mean + (1.0 - beta_first) * grads
    variance = beta_second * square + (1.0 - beta_second) * grads * grads
    update = moment / correct_first / (jnp.sqrt(variance / correct_second) + epsilon)
    master = params - learn_rate * (update + decay_rate * params)
    return (master, moment, variance)


def update_kernel(limit, entry_width, refs):
    squares_ref, total_ref = refs[:2]
    states, outs = refs[2:8], refs[8:]
    clip = clip_of(squares_ref, limit)
    for side, start in ((0, 0), (1, entry_width)):
        params_ref, mean_ref, square_ref = states[side], states[2 + side], states[4 + side]
        for c in range(0, params_ref.shape[2], 2 * LANES):
            cols = slice(c, c + 2 * LANES)
            there = slice(start + c, start + c + 2 * LANES)
            stepped = adamw_step(
                params_ref[0, :, cols],
                mean_ref[0, :, cols],
                square_ref[0, :, cols],
                total_ref[:, there],
                clip,
            )
            for kind, values in enumerate(stepped):
                outs[2 * kind + side][0, :, cols] = values


def update(squares, total, states, limit, entry_width):
    shapes = [jax.ShapeDtypeStruct(s.shape, s.dtype) for s in states]
    return pl.pallas_call(
        lambda *refs: update_kernel(limit, entry_width, refs),
        out_shape=shapes,
        name="own_state",
    )(squares, total, *states)


def share(rounded, entry_width):
    groups = lax.axis_size("group")
    own, width = rounded.shape
    far = groups // NEAR
    strides = [[r + NEAR * a for a in range(far)] for r in range(NEAR)]
    gathered = lax.all_gather(rounded, "group", axis=0, tiled=True, axis_index_groups=strides)

    def moved(values, by):
        return lax.ppermute(values, "group", [(i, (i + by) % groups) for i in range(groups)])

    ahead, behind = moved(gathered, -1), moved(gathered, 1)
    across = (moved(gathered[:, :entry_width], 2), moved(gathered[:, entry_width:], -2))
    me = lax.axis_index("group").astype(jnp.uint32)

    def placed(start, middle):
        cols = middle.shape[1]
        shape = (far, NEAR, own, cols)
        residue = lax.broadcasted_iota(jnp.uint32, shape, 1)

        def spread(values):
            return values.reshape(far, 1, own, values.shape[1])

        nearby = (spread(gathered), spread(ahead), None, spread(behind))
        out = spread(middle)
        for turn in (0, 1, 3):
            here = residue == ((me + turn) & (NEAR - 1))
            out = jnp.where(here, nearby[turn][..., start : start + cols], out)
        return out.reshape(groups * own, cols)

    return gathered, [placed(0, across[0]), placed(entry_width, across[1])]


def body(
    entry_grads,
    exit_grads,
    entry_params,
    exit_params,
    entry_mean,
    exit_mean,
    entry_square,
    exit_square,
):
    rows, entry_width = entry_grads.shape[2:]
    exit_width = exit_grads.shape[3]
    own = entry_params.shape[1]
    shards = lax.axis_size("shard")
    pieces = pieces_of(entry_grads.reshape(rows, entry_width), ENTRY_PIECE)
    pieces += pieces_of(exit_grads.reshape(rows, exit_width), EXIT_PIECE)
    places = places_of(rows, entry_width, ENTRY_PIECE, 0)
    places += places_of(rows, exit_width, EXIT_PIECE, entry_width)
    summed = lax.psum(pieces, "group")
    total, lanes = own_and_squares(summed, places, own, entry_width + exit_width, shards)
    squares = lax.all_to_all(lanes, "shard", 0, 0)
    limit = ((rows * entry_width + rows * exit_width) * shards) ** 0.5
    states = (entry_params, exit_params, entry_mean, exit_mean, entry_square, exit_square)
    packed = [jnp.concatenate([states[k][0], states[k + 1][0]], axis=1) for k in (0, 2, 4)]
    clip = jnp.minimum(jnp.float32(1.0), limit / (jnp.sqrt(jnp.sum(squares)) + 1e-06))
    rounded = adamw_step(*packed, total, clip)[0].astype(jnp.bfloat16)
    gathered, (entry_weights, exit_weights) = share(rounded, entry_width)
    squares, gathered = lax.optimization_barrier((squares, gathered))
    outs = update(squares, total, states, limit, entry_width)
    return (*outs, entry_weights[None], exit_weights[None])


def solution(mesh):
    placed = (
        P("group", "shard", None, None),
        P("group", "shard", None, None),
        P("shard", "group", None),
        P("shard", "group", None),
        P("shard", "group", None),
        P("shard", "group", None),
        P("shard", "group", None),
        P("shard", "group", None),
    )
    return jax.shard_map(
        body,
        mesh=mesh,
        in_specs=placed,
        out_specs=(
            P("shard", "group", None),
            P("shard", "group", None),
            P("shard", "group", None),
            P("shard", "group", None),
            P("shard", "group", None),
            P("shard", "group", None),
            P("shard", None, None),
            P("shard", None, None),
        ),
        check_vma=False,
    )
```

```python
import jax
import jax.numpy as jnp
from jax import lax
from jax.experimental import pallas as pl
from jax.experimental.pallas import tpu as pltpu
from jax.sharding import PartitionSpec as P

beta_first = 0.9
beta_second = 0.95
learn_rate = 0.01
decay_rate = 0.1
epsilon = 1e-08
correct_first = 1.0 - 0.9**40
correct_second = 1.0 - 0.95**40

LANES = 128
TILE = 8
NEAR = 4


def cuts_of(rows, width, splits):
    cuts = []
    for top in range(0, rows, TILE):
        wide = width // 2 if top < splits * TILE else width
        cuts += [(top, col, wide) for col in range(0, width, wide)]
    return cuts


def pieces_of(grads, cuts):
    return [grads[r : r + TILE, c : c + wide] for r, c, wide in cuts]


def own_and_squares_kernel(places, own, me_ref, *refs):
    piece_refs, (own_ref, lanes_ref) = refs[: len(places)], refs[len(places) :]
    me = me_ref[0, 0]
    sums = [jnp.zeros((TILE, LANES), jnp.float32) for _ in range(4)]
    turn = 0
    for piece_ref in piece_refs:
        for c in range(0, piece_ref.shape[1], LANES):
            values = piece_ref[:, c : c + LANES]
            sums[turn % 4] = sums[turn % 4] + values * values
            turn += 1
    sums = (sums[0] + sums[1]) + (sums[2] + sums[3])
    lanes = jnp.sum(sums, axis=0, keepdims=True)
    lanes_ref[...] = jnp.broadcast_to(lanes[None], lanes_ref.shape)
    for block in sorted({row // own for row, _ in places}):

        @pl.when(me == block)
        def _(block=block):
            for (row, col), piece_ref in zip(places, piece_refs):
                if row // own == block:
                    top = row - block * own
                    own_ref[top : top + TILE, col : col + piece_ref.shape[1]] = piece_ref[...]


def own_and_squares(pieces, places, own, width, shards):
    me = lax.axis_index("group").reshape(1, 1)
    return pl.pallas_call(
        lambda *refs: own_and_squares_kernel(places, own, *refs),
        in_specs=[pl.BlockSpec(memory_space=pltpu.SMEM)]
        + [pl.BlockSpec(memory_space=pltpu.VMEM) for _ in pieces],
        out_shape=(
            jax.ShapeDtypeStruct((own, width), jnp.float32),
            jax.ShapeDtypeStruct((shards, 1, LANES), jnp.float32),
        ),
        name="own_and_squares",
    )(me, *pieces)


def clip_of(squares_ref, limit):
    squares = jnp.sum(jnp.sum(squares_ref[...], axis=0), axis=1, keepdims=True)
    return jnp.minimum(jnp.float32(1.0), limit / (jnp.sqrt(squares) + 1e-06))


def adamw_step(params, mean, square, total, clip):
    grads = clip * total
    moment = beta_first * mean + (1.0 - beta_first) * grads
    variance = beta_second * square + (1.0 - beta_second) * grads * grads
    update = moment / correct_first / (jnp.sqrt(variance / correct_second) + epsilon)
    master = params - learn_rate * (update + decay_rate * params)
    return (master, moment, variance)


def update_kernel(limit, entry_width, refs):
    squares_ref, total_ref = refs[:2]
    states, outs = refs[2:8], refs[8:]
    clip = clip_of(squares_ref, limit)
    for side, start in ((0, 0), (1, entry_width)):
        params_ref, mean_ref, square_ref = states[side], states[2 + side], states[4 + side]
        for c in range(0, params_ref.shape[2], 2 * LANES):
            cols = slice(c, c + 2 * LANES)
            there = slice(start + c, start + c + 2 * LANES)
            stepped = adamw_step(
                params_ref[0, :, cols],
                mean_ref[0, :, cols],
                square_ref[0, :, cols],
                total_ref[:, there],
                clip,
            )
            for kind, values in enumerate(stepped):
                outs[2 * kind + side][0, :, cols] = values


def update(squares, total, states, limit, entry_width):
    shapes = [jax.ShapeDtypeStruct(s.shape, s.dtype) for s in states]
    return pl.pallas_call(
        lambda *refs: update_kernel(limit, entry_width, refs),
        out_shape=shapes,
        name="own_state",
    )(squares, total, *states)


def share(rounded, entry_width):
    groups = lax.axis_size("group")
    own, width = rounded.shape
    far = groups // NEAR
    strides = [[r + NEAR * a for a in range(far)] for r in range(NEAR)]
    gathered = lax.all_gather(rounded, "group", axis=0, tiled=True, axis_index_groups=strides)

    def moved(values, by):
        return lax.ppermute(values, "group", [(i, (i + by) % groups) for i in range(groups)])

    ahead, behind = moved(gathered, -1), moved(gathered, 1)
    across = (moved(gathered[:, :entry_width], 2), moved(gathered[:, entry_width:], -2))
    me = lax.axis_index("group").astype(jnp.uint32)

    def placed(start, middle):
        cols = middle.shape[1]
        shape = (far, NEAR, own, cols)
        residue = lax.broadcasted_iota(jnp.uint32, shape, 1)

        def spread(values):
            return values.reshape(far, 1, own, values.shape[1])

        nearby = (spread(gathered), spread(ahead), None, spread(behind))
        out = spread(middle)
        for turn in (0, 1, 3):
            here = residue == ((me + turn) & (NEAR - 1))
            out = jnp.where(here, nearby[turn][..., start : start + cols], out)
        return out.reshape(groups * own, cols)

    return gathered, [placed(0, across[0]), placed(entry_width, across[1])]


def body(
    entry_grads,
    exit_grads,
    entry_params,
    exit_params,
    entry_mean,
    exit_mean,
    entry_square,
    exit_square,
):
    rows, entry_width = entry_grads.shape[2:]
    exit_width = exit_grads.shape[3]
    own = entry_params.shape[1]
    shards = lax.axis_size("shard")
    entry_cuts, exit_cuts = cuts_of(rows, entry_width, 0), cuts_of(rows, exit_width, 1)
    entry_local = entry_grads.reshape(rows, entry_width)
    exit_pieces = pieces_of(exit_grads.reshape(rows, exit_width), exit_cuts)
    pieces = pieces_of(entry_local, entry_cuts) + exit_pieces
    places = [(r, c) for r, c, _ in entry_cuts] + [(r, entry_width + c) for r, c, _ in exit_cuts]
    summed = lax.psum(pieces, "group")
    total, lanes = own_and_squares(summed, places, own, entry_width + exit_width, shards)
    squares = lax.all_to_all(lanes, "shard", 0, 0)
    limit = ((rows * entry_width + rows * exit_width) * shards) ** 0.5
    states = (entry_params, exit_params, entry_mean, exit_mean, entry_square, exit_square)
    packed = [jnp.concatenate([states[k][0], states[k + 1][0]], axis=1) for k in (0, 2, 4)]
    clip = jnp.minimum(jnp.float32(1.0), limit / (jnp.sqrt(jnp.sum(squares)) + 1e-06))
    rounded = adamw_step(*packed, total, clip)[0].astype(jnp.bfloat16)
    gathered, (entry_weights, exit_weights) = share(rounded, entry_width)
    squares, gathered = lax.optimization_barrier((squares, gathered))
    outs = update(squares, total, states, limit, entry_width)
    return (*outs, entry_weights[None], exit_weights[None])


def solution(mesh):
    placed = (
        P("group", "shard", None, None),
        P("group", "shard", None, None),
        P("shard", "group", None),
        P("shard", "group", None),
        P("shard", "group", None),
        P("shard", "group", None),
        P("shard", "group", None),
        P("shard", "group", None),
    )
    return jax.shard_map(
        body,
        mesh=mesh,
        in_specs=placed,
        out_specs=(
            P("shard", "group", None),
            P("shard", "group", None),
            P("shard", "group", None),
            P("shard", "group", None),
            P("shard", "group", None),
            P("shard", "group", None),
            P("shard", None, None),
            P("shard", None, None),
        ),
        check_vma=False,
    )
```

```python
import jax
import jax.numpy as jnp
from jax import lax
from jax.experimental import pallas as pl
from jax.experimental.pallas import tpu as pltpu
from jax.sharding import PartitionSpec as P

beta_first = 0.9
beta_second = 0.95
learn_rate = 0.01
decay_rate = 0.1
epsilon = 1e-08
correct_first = 1.0 - 0.9**40
correct_second = 1.0 - 0.95**40

LANES = 128
TILE = 8
NEAR = 4


def cuts_of(rows, width, splits):
    cuts = []
    for top in range(0, rows, TILE):
        wide = width // 2 if top < splits * TILE else width
        cuts += [(top, col, wide) for col in range(0, width, wide)]
    return cuts


def pieces_of(grads, cuts):
    return [grads[r : r + TILE, c : c + wide] for r, c, wide in cuts]


def own_and_squares_kernel(places, own, me_ref, *refs):
    piece_refs, (own_ref, lanes_ref) = refs[: len(places)], refs[len(places) :]
    me = me_ref[0, 0]
    sums = [jnp.zeros((TILE, LANES), jnp.float32) for _ in range(4)]
    turn = 0
    for piece_ref in piece_refs:
        for c in range(0, piece_ref.shape[1], LANES):
            values = piece_ref[:, c : c + LANES]
            sums[turn % 4] = sums[turn % 4] + values * values
            turn += 1
    sums = (sums[0] + sums[1]) + (sums[2] + sums[3])
    lanes = jnp.sum(sums, axis=0, keepdims=True)
    lanes_ref[...] = jnp.broadcast_to(lanes[None], lanes_ref.shape)
    for block in sorted({row // own for row, _ in places}):

        @pl.when(me == block)
        def _(block=block):
            for (row, col), piece_ref in zip(places, piece_refs):
                if row // own == block:
                    top = row - block * own
                    own_ref[top : top + TILE, col : col + piece_ref.shape[1]] = piece_ref[...]


def own_and_squares(pieces, places, own, width, shards):
    me = lax.axis_index("group").reshape(1, 1)
    return pl.pallas_call(
        lambda *refs: own_and_squares_kernel(places, own, *refs),
        in_specs=[pl.BlockSpec(memory_space=pltpu.SMEM)]
        + [pl.BlockSpec(memory_space=pltpu.VMEM) for _ in pieces],
        out_shape=(
            jax.ShapeDtypeStruct((own, width), jnp.float32),
            jax.ShapeDtypeStruct((shards, 1, LANES), jnp.float32),
        ),
        name="own_and_squares",
    )(me, *pieces)


def clip_of(squares_ref, limit):
    squares = jnp.sum(jnp.sum(squares_ref[...], axis=0), axis=1, keepdims=True)
    return jnp.minimum(jnp.float32(1.0), limit / (jnp.sqrt(squares) + 1e-06))


def adamw_step(params, mean, square, total, clip):
    grads = clip * total
    moment = beta_first * mean + (1.0 - beta_first) * grads
    variance = beta_second * square + (1.0 - beta_second) * grads * grads
    update = moment / correct_first / (jnp.sqrt(variance / correct_second) + epsilon)
    master = params - learn_rate * (update + decay_rate * params)
    return (master, moment, variance)


def update_kernel(limit, entry_width, refs):
    squares_ref, total_ref = refs[:2]
    states, outs = refs[2:8], refs[8:]
    clip = clip_of(squares_ref, limit)
    for side, start in ((0, 0), (1, entry_width)):
        params_ref, mean_ref, square_ref = states[side], states[2 + side], states[4 + side]
        for c in range(0, params_ref.shape[2], 2 * LANES):
            cols = slice(c, c + 2 * LANES)
            there = slice(start + c, start + c + 2 * LANES)
            stepped = adamw_step(
                params_ref[0, :, cols],
                mean_ref[0, :, cols],
                square_ref[0, :, cols],
                total_ref[:, there],
                clip,
            )
            for kind, values in enumerate(stepped):
                outs[2 * kind + side][0, :, cols] = values


def update(squares, total, states, limit, entry_width):
    shapes = [jax.ShapeDtypeStruct(s.shape, s.dtype) for s in states]
    return pl.pallas_call(
        lambda *refs: update_kernel(limit, entry_width, refs),
        out_shape=shapes,
        name="own_state",
    )(squares, total, *states)


def share(rounded, entry_width):
    groups = lax.axis_size("group")
    own, width = rounded.shape
    far = groups // NEAR
    strides = [[r + NEAR * a for a in range(far)] for r in range(NEAR)]
    gathered = lax.all_gather(rounded, "group", axis=0, tiled=True, axis_index_groups=strides)

    def moved(values, by):
        return lax.ppermute(values, "group", [(i, (i + by) % groups) for i in range(groups)])

    ahead, behind = moved(gathered, -1), moved(gathered, 1)
    cut = entry_width // 2
    left, right = moved(gathered[:, :cut], 2), moved(gathered[:, cut:], -2)
    across = (jnp.concatenate([left, right[:, :cut]], axis=1), right[:, cut:])
    me = lax.axis_index("group").astype(jnp.uint32)

    def placed(nearby, cols):
        shape = (far, NEAR, own, cols)
        residue = lax.broadcasted_iota(jnp.uint32, shape, 1)
        out = nearby[0].reshape(far, 1, own, cols)
        for turn in range(1, NEAR):
            here = residue == ((me + turn) & (NEAR - 1))
            out = jnp.where(here, nearby[turn].reshape(far, 1, own, cols), out)
        return out.reshape(groups * own, cols)

    sides = ((slice(0, entry_width), across[0]), (slice(entry_width, width), across[1]))
    return gathered, [
        placed((gathered[:, cols], ahead[:, cols], middle, behind[:, cols]), middle.shape[1])
        for cols, middle in sides
    ]


def body(
    entry_grads,
    exit_grads,
    entry_params,
    exit_params,
    entry_mean,
    exit_mean,
    entry_square,
    exit_square,
):
    rows, entry_width = entry_grads.shape[2:]
    exit_width = exit_grads.shape[3]
    own = entry_params.shape[1]
    shards = lax.axis_size("shard")
    entry_cuts, exit_cuts = cuts_of(rows, entry_width, 0), cuts_of(rows, exit_width, 1)
    entry_local = entry_grads.reshape(rows, entry_width)
    exit_pieces = pieces_of(exit_grads.reshape(rows, exit_width), exit_cuts)
    pieces = pieces_of(entry_local, entry_cuts) + exit_pieces
    places = [(r, c) for r, c, _ in entry_cuts] + [(r, entry_width + c) for r, c, _ in exit_cuts]
    summed = lax.psum(pieces, "group")
    total, lanes = own_and_squares(summed, places, own, entry_width + exit_width, shards)
    squares = lax.all_to_all(lanes, "shard", 0, 0)
    limit = ((rows * entry_width + rows * exit_width) * shards) ** 0.5
    states = (entry_params, exit_params, entry_mean, exit_mean, entry_square, exit_square)
    packed = [jnp.concatenate([states[k][0], states[k + 1][0]], axis=1) for k in (0, 2, 4)]
    clip = jnp.minimum(jnp.float32(1.0), limit / (jnp.sqrt(jnp.sum(squares)) + 1e-06))
    rounded = adamw_step(*packed, total, clip)[0].astype(jnp.bfloat16)
    gathered, (entry_weights, exit_weights) = share(rounded, entry_width)
    squares, gathered = lax.optimization_barrier((squares, gathered))
    outs = update(squares, total, states, limit, entry_width)
    return (*outs, entry_weights[None], exit_weights[None])


def solution(mesh):
    placed = (
        P("group", "shard", None, None),
        P("group", "shard", None, None),
        P("shard", "group", None),
        P("shard", "group", None),
        P("shard", "group", None),
        P("shard", "group", None),
        P("shard", "group", None),
        P("shard", "group", None),
    )
    return jax.shard_map(
        body,
        mesh=mesh,
        in_specs=placed,
        out_specs=(
            P("shard", "group", None),
            P("shard", "group", None),
            P("shard", "group", None),
            P("shard", "group", None),
            P("shard", "group", None),
            P("shard", "group", None),
            P("shard", None, None),
            P("shard", None, None),
        ),
        check_vma=False,
    )
```
